32 devices in a mesh: snap: 2 (over x), row: 16 (over z, y, core).
Axes of the slice: x: 2, y: 2, z: 4, core: 2. Of those that a mesh axis runs over, the one named last changes fastest.
Arguments:
- snapshots: bfloat16 [256, 262144], P('snap', 'row'), may hold values from -64 to 64
- counts: int32 [16], P('row'), may hold values from 1 to 16384, 196608 in all
Outputs:
- basis: bfloat16 [256, 262144], P('snap', 'row')
- r_factor: float32 [256, 256], replicated
The draws below stay inside these ranges and needn't reach their ends.
Inputs may be any that keep to these rules, and one draw needn't show every extreme that they name: `counts`: at least one row and at most 16384 rows are live on each index of row, and some index has all 16384 live.
All inputs are finite; a program needn't handle non-finite values. No bound on the sum of `counts` on one device may be relied on, other than what follows from the above.
Results may differ from the reference program's by a relative error of at most 0.0049.
Values may be sent and summed in bfloat16 or wider, within the bound.
A program may use at most 64 MiB of HBM per device.

```python
import math
import jax
import jax.numpy as jnp
import numpy as np
from jax import lax

K = 256
ROWS_DEV = 16384
NROWS = 262144
N_ROW = 16


def draw_snapshots(key, part):
    keys = jax.random.split(key, 2)
    row_scale = jnp.exp(jax.random.uniform(keys[1], (1, NROWS), jnp.float32, 0.0, math.log(10.0)))
    base = jnp.clip(jax.random.normal(keys[0], (K, NROWS), jnp.float32), -5.0, 5.0)
    values = base * row_scale
    return values.astype(jnp.bfloat16)


def profile(number_of, total, limit, skew):
    portions = [(1 << 20) // math.isqrt(grade ** skew) + 1 for grade in range(2, number_of + 1)]
    rest, given = total - limit - (number_of - 1), [1] * (number_of - 1)
    while rest > 0:
        candidates = [i for i in range(number_of - 1) if given[i] < limit]
        mass, budget = sum([portions[i] for i in candidates]), rest
        for i in candidates:
            extra = min(limit - given[i], max(1, budget * portions[i] // mass), rest)
            given[i] = given[i] + extra
            rest = rest - extra
    return np.array([limit] + given)


def ragged(stream_key, amount, total, most, skew):
    if amount == 2:
        one = jax.random.randint(stream_key, (), max(1, total - most), min(most, total - 1) + 1)
        return jnp.stack([one, total - one])
    sizes = jnp.asarray(profile(amount, total, most, skew), jnp.int32)
    twos = (amount - 1) // 2
    source_of, receiver = sizes[1:1 + 2 * twos:2], sizes[2:2 + 2 * twos:2]
    room = jnp.minimum(source_of - 1, most - receiver)
    moved = jax.random.randint(jax.random.fold_in(stream_key, 1), (twos,), 0, 1 << 20) % (room + 1)
    sizes = sizes.at[1:1 + 2 * twos:2].set(source_of - moved).at[2:2 + 2 * twos:2].set(receiver + moved)
    return sizes[jax.random.permutation(jax.random.fold_in(stream_key, 2), amount)]


def setup_inputs(seed: int = 0) -> dict:
    splits = jax.random.split(jax.random.key(seed), 3)
    return {
        "snapshots": draw_snapshots(jax.random.fold_in(splits[2], 71), 0),
        "counts": ragged(splits[1], N_ROW, N_ROW * ROWS_DEV * 3 // 4, ROWS_DEV, 1).astype(jnp.int32),
    }


def reference(snapshots, counts):
    blocks = jnp.transpose(snapshots.reshape(K, N_ROW, ROWS_DEV), (1, 0, 2))
    slot = lax.broadcasted_iota(jnp.int32, (1, ROWS_DEV), 1)

    def masked(block, count):
        return jnp.where(slot < count, block, jnp.zeros_like(block))

    def add_gram(total, item):
        block, count = item
        live = masked(block, count)
        term = lax.dot_general(live.astype(jnp.float32), live.astype(jnp.float32), (((1,), (1,)), ((), ())), preferred_element_type=jnp.float32)
        return (total + term, 0)
    gram, _ = lax.scan(add_gram, jnp.zeros((K, K), jnp.float32), (blocks, counts))
    lower = jnp.linalg.cholesky(gram)
    scale = math.sqrt(NROWS)
    r_factor = lower.T / scale
    inverse = lax.linalg.triangular_solve(lower, jnp.eye(K, dtype=jnp.float32), left_side=True, lower=True).T
    weights = (inverse * scale).astype(jnp.bfloat16)

    def form(item):
        block, count = item
        live = masked(block, count)
        return lax.dot_general(weights.astype(jnp.float32), live.astype(jnp.float32), (((0,), (0,)), ((), ())), preferred_element_type=jnp.float32).astype(jnp.bfloat16)
    formed = lax.map(form, (blocks, counts))
    basis = jnp.transpose(formed, (1, 0, 2)).reshape(K, NROWS)
    return (basis, r_factor)
```

```python
import functools
import math

import jax
import jax.numpy as jnp
from jax import lax
from jax.experimental import pallas as pl
from jax.experimental.pallas import tpu as pltpu
from jax.sharding import PartitionSpec as P

MESH = pl.DeviceIdType.MESH
HIGH = lax.Precision.HIGHEST
LANES = 128
SUBLANES = 8


def gram_of(block):
    return lax.dot_general(
        block, block, (((1,), (1,)), ((), ())), preferred_element_type=jnp.float32
    )


def factors(gram, scale):
    lower = jnp.linalg.cholesky(gram)
    r_factor = lower.T / scale
    width = gram.shape[0]
    inverse = lax.linalg.triangular_solve(
        lower, jnp.eye(width, dtype=jnp.float32), left_side=True, lower=True
    ).T
    weights = (inverse * scale).astype(jnp.bfloat16)
    return (r_factor, weights)


def apply_weights(weights, block):
    return lax.dot_general(
        weights, block, (((0,), (0,)), ((), ())), preferred_element_type=jnp.float32
    ).astype(jnp.bfloat16)


def shards(snapshots, counts):
    narrow, slots = snapshots.shape
    slot = lax.broadcasted_iota(jnp.int32, (1, slots), 1)
    live = jnp.where(slot < counts[0], snapshots, jnp.zeros_like(snapshots))
    scale = math.sqrt(slots * lax.axis_size("row"))
    whole = lax.all_gather(live, "snap", axis=0, tiled=True)
    gram = lax.psum(gram_of(whole), "row")
    r_factor, weights = factors(gram, scale)
    start = lax.axis_index("snap") * narrow
    own_weights = lax.dynamic_slice_in_dim(weights, start, narrow, 1)
    basis = apply_weights(own_weights, whole)
    return (basis, r_factor)


def mxu_nt(a, b):
    return lax.dot_general(
        a, b, (((1,), (1,)), ((), ())), preferred_element_type=jnp.float32
    )


def eliminate(groups):
    shape = groups[0].shape
    tall = shape[0]
    lane = lax.broadcasted_iota(jnp.int32, shape, 1)
    sub = lax.broadcasted_iota(jnp.int32, shape, 0)
    groups = list(groups)
    count = len(groups)

    def line(block, p):
        return jnp.broadcast_to(block[p:p + 1, :], shape)

    for g in range(count):
        columns = [
            [
                jnp.broadcast_to(groups[v][:, g * tall + q:g * tall + q + 1], shape)
                for v in range(g, count)
            ]
            for q in range(tall)
        ]
        for p in range(tall):
            here = lane == g * tall + p
            pivot = line(columns[p][0], p)
            root = lax.rsqrt(pivot)
            root = root * (1.5 - 0.5 * pivot * root * root)
            lefts = [column * root for column in columns[p]]
            lefts[0] = jnp.where(sub > p, lefts[0], 0.0)
            for q in range(p + 1, tall):
                top = line(columns[q][0], p) * root
                columns[q] = [c - m * top for c, m in zip(columns[q], lefts)]
            row = jnp.where(here, root, line(groups[g], p) * root)
            for v in range(g, count):
                old = groups[v]
                new = jnp.where(here, 0.0, old) - lefts[v - g] * row
                if v == g:
                    new = jnp.where(sub == p, row, jnp.where(sub > p, new, old))
                groups[v] = new
    return groups


def factor_body(scale, gram_ref, r_ref, own_ref, other_ref, work, roots):
    narrow = gram_ref.shape[2]
    rows = narrow // 2
    snap = lax.axis_index("snap")
    row = lax.broadcasted_iota(jnp.int32, (narrow, narrow), 0)
    col = lax.broadcasted_iota(jnp.int32, (narrow, narrow), 1)

    def gram(i):
        here = slice(i * rows, (i + 1) * rows)
        return jnp.concatenate([gram_ref[0, here, :], gram_ref[1, here, :]], axis=0)

    def dot(a, b, dims):
        return lax.dot_general(
            a, b, (dims, ((), ())), precision=HIGH, preferred_element_type=jnp.float32
        )

    def diagonal(which):
        full = work[which]
        inverse = jnp.where(col <= row, full, 0.0)
        upper = jnp.where(col > row, full, 0.0)
        upper = jnp.where(col == row, 1.0 / full, upper)
        return inverse, upper

    work[0] = gram(0)
    work[1] = gram(1)

    @pl.loop(0, 2)
    def _(block):
        groups = [
            work[block, SUBLANES * v:SUBLANES * (v + 1), :] for v in range(narrow // SUBLANES)
        ]
        for v, group in enumerate(eliminate(groups)):
            work[block, SUBLANES * v:SUBLANES * (v + 1), :] = group

        @pl.when(block == 0)
        def _():
            inverse, _ = diagonal(0)
            right = dot(inverse, gram(2), ((1,), (0,)))
            roots[...] = right
            work[1] = work[1] - dot(right, right, ((0,), (0,)))

    inverse0, upper0 = diagonal(0)
    inverse1, upper1 = diagonal(1)
    right = roots[...]
    below = -dot(inverse1, dot(right, inverse0, ((0,), (0,))), ((1,), (0,)))
    r_ref[0:narrow, 0:narrow] = upper0 / scale
    r_ref[0:narrow, narrow:] = right / scale
    r_ref[narrow:, 0:narrow] = jnp.zeros_like(right)
    r_ref[narrow:, narrow:] = upper1 / scale
    own = jnp.where(snap == 0, inverse0, inverse1)
    own_ref[...] = (own * scale).astype(own_ref.dtype)
    other = jnp.where(snap == 0, 0.0, below)
    other_ref[...] = (other * scale).astype(other_ref.dtype)


def meet(sem, stage, chip_row, core):
    y, z = lax.rem(chip_row, 2), lax.div(chip_row, 2)
    last = lax.axis_size("row") // 4 - 1

    def signal(chip):
        pl.semaphore_signal(
            sem.at[stage], inc=1, device_id={"row": 2 * chip + core}, device_id_type=MESH
        )

    signal(chip_row + 1 - 2 * y)

    @pl.when(z > 0)
    def _():
        signal(chip_row - 2)

    @pl.when(z < last)
    def _():
        signal(chip_row + 2)


def meetings(chip_row):
    z = lax.div(chip_row, 2)
    last = lax.axis_size("row") // 4 - 1
    return 1 + jnp.where(z > 0, 1, 0) + jnp.where(z < last, 1, 0)


def panel_kernel(
    units, scale, counts_ref, x_ref, own, got, r_ref, own_w_ref, other_w_ref,
    mine, near, summed, theirs, part, parts, gram_ref, work, roots,
    load_sem, send_sem, recv_sem, met, near_send, near_recv, sum_send, sum_recv,
    part_send, part_recv, out_send, out_recv, pair_send, pair_recv,
):
    snap = lax.axis_index("snap")
    me = lax.axis_index("row")
    core, chip = lax.rem(me, 2), lax.div(me, 2)
    chips = lax.axis_size("row") // 2
    other = {"snap": 1 - snap}
    pair = {"row": me + 1 - 2 * core}
    narrow, slots = x_ref.shape
    step = slots // units
    halfway = units // 2
    half = slots // 2
    count = counts_ref[0]
    rows = narrow // 2
    y, z = lax.rem(chip, 2), lax.div(chip, 2)
    last = chips // 2 - 1

    barrier = pltpu.get_barrier_semaphore()

    def greet(device):
        pl.semaphore_signal(barrier, inc=1, device_id=device, device_id_type=MESH)

    greet(other)
    greet(pair)
    greet({"row": 2 * (chip + 1 - 2 * y) + core})

    @pl.when(z > 0)
    def _():
        greet({"row": me - 4})

    @pl.when(z < last)
    def _():
        greet({"row": me + 4})

    wide = 8
    span = slots // wide
    loads = []
    for c in range(wide):
        at = pl.ds(c * span, span)
        copy = pltpu.make_async_copy(x_ref.at[:, at], own.at[:, at], load_sem.at[c])
        copy.start()
        loads.append(copy)

    pl.semaphore_wait(barrier, 2 + meetings(chip))

    def bulk(u):
        at = pl.ds(u * step, step)
        return pltpu.make_async_remote_copy(
            src_ref=x_ref.at[:, at], dst_ref=got.at[:, at],
            send_sem=send_sem.at[u], recv_sem=recv_sem.at[u],
            device_id=other, device_id_type=MESH,
        )

    def send(low, high):
        @pl.when(snap == 0)
        def _():
            for u in range(low, high):
                bulk(u).start()

        top = min(high, halfway)

        @pl.when(snap == 1)
        def _():
            for u in range(low, top):
                bulk(halfway + u).start()

    send(0, 6)

    def masked(block, start):
        lane = lax.broadcasted_iota(jnp.int32, block.shape, 1) + start
        return jnp.where(lane < count, block, jnp.zeros_like(block))

    total = jnp.zeros((narrow, narrow), jnp.float32)
    for c in range(wide):
        loads[c].wait()
        block = own[:, c * span:(c + 1) * span]
        total = total + mxu_nt(masked(block, c * span), block)
    mine[0] = total

    def near_copy(i):
        return pltpu.make_async_remote_copy(
            src_ref=mine.at[i, pl.ds(pl.multiple_of((1 - core) * rows, SUBLANES), rows)],
            dst_ref=near.at[i],
            send_sem=near_send.at[i], recv_sem=near_recv.at[i],
            device_id=pair, device_id_type=MESH,
        )

    def sum_copy(i):
        away = near_copy(i)
        away.start()
        away.wait()
        kept = mine[i, pl.ds(pl.multiple_of(core * rows, SUBLANES), rows), :]
        summed[i] = kept + near[i]
        return pltpu.make_async_remote_copy(
            src_ref=summed.at[i], dst_ref=theirs.at[i],
            send_sem=sum_send.at[i], recv_sem=sum_recv.at[i],
            device_id=other, device_id_type=MESH,
        )

    diagonal = sum_copy(0)
    diagonal.start()
    send(6, halfway + 1)

    for stage in range(met.shape[0]):
        meet(met, stage, chip, core)
        pl.semaphore_wait(met.at[stage], meetings(chip))

    mine[1] = jnp.zeros((narrow, narrow), jnp.float32)
    for u in range(halfway):
        @pl.when(snap == 1)
        def _():
            bulk(u).wait_recv()
            start = u * step
            block = masked(own[:, start:start + step], start)
            mine[1] = mine[1] + mxu_nt(got[:, start:start + step], block)

        @pl.when(snap == 0)
        def _():
            bulk(halfway + u).wait_recv()
            start = half + u * step
            block = masked(own[:, start:start + step], start)
            mine[1] = mine[1] + mxu_nt(block, got[:, start:start + step])

    crossed = sum_copy(1)
    crossed.start()
    send(halfway + 1, units)

    diagonal.wait()
    part[0:rows, :] = jnp.where(snap == 0, summed[0], theirs[0])
    part[rows:2 * rows, :] = jnp.where(snap == 0, theirs[0], summed[0])
    crossed.wait()
    part[2 * rows:3 * rows, :] = summed[1] + theirs[1]

    lines = part.shape[0] // chips

    def at(i):
        return pl.ds(pl.multiple_of(i * lines, SUBLANES), lines)

    copies = []
    for d in range(1, chips):
        peer = lax.rem(chip + d, chips)
        copy = pltpu.make_async_remote_copy(
            src_ref=part.at[at(peer)], dst_ref=parts.at[d - 1],
            send_sem=part_send.at[d - 1], recv_sem=part_recv.at[d - 1],
            device_id={"row": 2 * peer + core}, device_id_type=MESH,
        )
        copy.start()
        copies.append(copy)
    total = part[at(chip), :]
    for d in range(1, chips):
        copies[d - 1].wait_recv()
        total = total + parts[d - 1]
    gram_ref[core, at(chip), :] = total
    results = []
    for d in range(1, 2 * chips):
        peer = lax.rem(me + d, 2 * chips)
        copy = pltpu.make_async_remote_copy(
            src_ref=gram_ref.at[core, at(chip)], dst_ref=gram_ref.at[core, at(chip)],
            send_sem=out_send.at[d - 1], recv_sem=out_recv.at[d - 1],
            device_id={"row": peer}, device_id_type=MESH,
        )
        copy.start()
        results.append(copy)
    for copy in copies:
        copy.wait_send()
    for copy in results:
        copy.wait()

    factor_body(scale, gram_ref, r_ref, own_w_ref, other_w_ref, work, roots)

    @pl.when(snap == 0)
    def _():
        for u in range(units):
            bulk(u).wait_send()

    @pl.when(snap == 1)
    def _():
        for u in range(halfway, units):
            bulk(u).wait_send()
        for u in range(halfway, units):
            bulk(u).wait_recv()


def exchange_and_factor(snapshots, counts, scale, units=32):
    narrow, slots = snapshots.shape
    dtype = snapshots.dtype
    n = lax.axis_size("row")
    chips = n // 2
    rows = narrow // 2
    height = 3 * rows
    f32 = jnp.float32
    vmem = pl.BlockSpec(memory_space=pltpu.VMEM)
    dma = pltpu.SemaphoreType.DMA
    return pl.pallas_call(
        functools.partial(panel_kernel, units, scale),
        name="exchange_and_factor",
        out_shape=(
            jax.ShapeDtypeStruct((narrow, slots), dtype),
            jax.ShapeDtypeStruct((narrow, slots), dtype),
            jax.ShapeDtypeStruct((2 * narrow, 2 * narrow), f32),
            jax.ShapeDtypeStruct((narrow, narrow), dtype),
            jax.ShapeDtypeStruct((narrow, narrow), dtype),
        ),
        in_specs=[
            pl.BlockSpec(memory_space=pltpu.SMEM),
            pl.BlockSpec(memory_space=pltpu.HBM),
        ],
        out_specs=(vmem, vmem, vmem, vmem, vmem),
        scratch_shapes=[
            pltpu.VMEM((2, narrow, narrow), f32),
            pltpu.VMEM((2, rows, narrow), f32),
            pltpu.VMEM((2, rows, narrow), f32),
            pltpu.VMEM((2, rows, narrow), f32),
            pltpu.VMEM((height, narrow), f32),
            pltpu.VMEM((chips - 1, height // chips, narrow), f32),
            pltpu.VMEM((2, height, narrow), f32),
            pltpu.VMEM((2, narrow, narrow), f32),
            pltpu.VMEM((narrow, narrow), f32),
            dma((8,)),
            dma((units,)),
            dma((units,)),
            pltpu.SemaphoreType.REGULAR((3,)),
            dma((2,)),
            dma((2,)),
            dma((2,)),
            dma((2,)),
            dma((chips - 1,)),
            dma((chips - 1,)),
            dma((n - 1,)),
            dma((n - 1,)),
            dma((1,)),
            dma((1,)),
        ],
        compiler_params=pltpu.CompilerParams(
            collective_id=0, has_side_effects=True, vmem_limit_bytes=44 << 20
        ),
    )(counts, snapshots)


def basis_kernel(pieces, counts_ref, own_w, other_w, r_in, own_ref, got_ref, out_ref, r_out, stage, sems):
    snap = lax.axis_index("snap")
    narrow, slots = own_ref.shape
    step = slots // pieces
    count = counts_ref[0]

    def piece(c):
        at = pl.ds(c * step, step)
        return pltpu.make_async_copy(stage.at[:, at], out_ref.at[:, at], sems.at[c])

    def form(weights, block, c):
        value = lax.dot_general(
            weights, block, (((1,), (0,)), ((), ())), preferred_element_type=jnp.float32
        )
        lane = lax.broadcasted_iota(jnp.int32, value.shape, 1) + c * step
        value = jnp.where(lane < count, value, 0.0).astype(stage.dtype)
        stage[:, c * step:(c + 1) * step] = value
        piece(c).start()

    @pl.when(snap == 0)
    def _():
        weights = own_w[...]
        for c in range(pieces):
            form(weights, own_ref[:, c * step:(c + 1) * step], c)

    @pl.when(snap == 1)
    def _():
        weights = jnp.concatenate([own_w[...], other_w[...]], axis=1)
        for c in range(pieces):
            here = slice(c * step, (c + 1) * step)
            form(weights, jnp.concatenate([own_ref[:, here], got_ref[:, here]], axis=0), c)

    r_out[...] = r_in[...]
    for c in range(pieces):
        piece(c).wait()


def form_basis(counts, own_w, other_w, r_factor, own, got, pieces=8):
    narrow, slots = own.shape
    vmem = pl.BlockSpec(memory_space=pltpu.VMEM)
    return pl.pallas_call(
        functools.partial(basis_kernel, pieces),
        name="form_basis",
        out_shape=(
            jax.ShapeDtypeStruct((narrow, slots), own.dtype),
            jax.ShapeDtypeStruct(r_factor.shape, r_factor.dtype),
        ),
        in_specs=[pl.BlockSpec(memory_space=pltpu.SMEM), vmem, vmem, vmem, vmem, vmem],
        out_specs=(pl.BlockSpec(memory_space=pltpu.HBM), vmem),
        scratch_shapes=[
            pltpu.VMEM((narrow, slots), own.dtype),
            pltpu.SemaphoreType.DMA((pieces,)),
        ],
        compiler_params=pltpu.CompilerParams(vmem_limit_bytes=16 << 20),
        cost_estimate=pl.CostEstimate(
            flops=4 * narrow * narrow * slots, bytes_accessed=8 * narrow * slots, transcendentals=0
        ),
    )(counts, own_w, other_w, r_factor, own, got)


def halves(snapshots, counts):
    slots = snapshots.shape[1]
    scale = math.sqrt(slots * lax.axis_size("row"))
    own, got, r_factor, own_w, other_w = exchange_and_factor(snapshots, counts, scale)
    return form_basis(counts, own_w, other_w, r_factor, own, got)


def two_halves(mesh):
    return mesh.shape["snap"] == 2 and mesh.shape["row"] == 16


def solution(mesh):
    placed = (P("snap", "row"), P("row"))
    body = halves if two_halves(mesh) else shards
    return jax.shard_map(
        body, mesh=mesh, in_specs=placed, out_specs=(P("snap", "row"), P()), check_vma=False
    )
```

```python
import functools
import math

import jax
import jax.numpy as jnp
from jax import lax
from jax.experimental import pallas as pl
from jax.experimental.pallas import tpu as pltpu
from jax.sharding import PartitionSpec as P

MESH = pl.DeviceIdType.MESH
HIGH = lax.Precision.HIGHEST
LANES = 128
SUBLANES = 8


def gram_of(block):
    return lax.dot_general(
        block, block, (((1,), (1,)), ((), ())), preferred_element_type=jnp.float32
    )


def factors(gram, scale):
    lower = jnp.linalg.cholesky(gram)
    r_factor = lower.T / scale
    width = gram.shape[0]
    inverse = lax.linalg.triangular_solve(
        lower, jnp.eye(width, dtype=jnp.float32), left_side=True, lower=True
    ).T
    weights = (inverse * scale).astype(jnp.bfloat16)
    return (r_factor, weights)


def apply_weights(weights, block):
    return lax.dot_general(
        weights, block, (((0,), (0,)), ((), ())), preferred_element_type=jnp.float32
    ).astype(jnp.bfloat16)


def shards(snapshots, counts):
    narrow, slots = snapshots.shape
    slot = lax.broadcasted_iota(jnp.int32, (1, slots), 1)
    live = jnp.where(slot < counts[0], snapshots, jnp.zeros_like(snapshots))
    scale = math.sqrt(slots * lax.axis_size("row"))
    whole = lax.all_gather(live, "snap", axis=0, tiled=True)
    gram = lax.psum(gram_of(whole), "row")
    r_factor, weights = factors(gram, scale)
    start = lax.axis_index("snap") * narrow
    own_weights = lax.dynamic_slice_in_dim(weights, start, narrow, 1)
    basis = apply_weights(own_weights, whole)
    return (basis, r_factor)


def mxu_nt(a, b):
    return lax.dot_general(
        a, b, (((1,), (1,)), ((), ())), preferred_element_type=jnp.float32
    )


def eliminate(groups):
    shape = groups[0].shape
    tall = shape[0]
    lane = lax.broadcasted_iota(jnp.int32, shape, 1)
    sub = lax.broadcasted_iota(jnp.int32, shape, 0)
    groups = list(groups)
    count = len(groups)

    def line(block, p):
        return jnp.broadcast_to(block[p:p + 1, :], shape)

    for g in range(count):
        columns = [
            [
                jnp.broadcast_to(groups[v][:, g * tall + q:g * tall + q + 1], shape)
                for v in range(g, count)
            ]
            for q in range(tall)
        ]
        for p in range(tall):
            here = lane == g * tall + p
            pivot = line(columns[p][0], p)
            root = lax.rsqrt(pivot)
            root = root * (1.5 - 0.5 * pivot * root * root)
            lefts = [column * root for column in columns[p]]
            lefts[0] = jnp.where(sub > p, lefts[0], 0.0)
            for q in range(p + 1, tall):
                top = line(columns[q][0], p) * root
                columns[q] = [c - m * top for c, m in zip(columns[q], lefts)]
            row = jnp.where(here, root, line(groups[g], p) * root)
            for v in range(g, count):
                old = groups[v]
                new = jnp.where(here, 0.0, old) - lefts[v - g] * row
                if v == g:
                    new = jnp.where(sub == p, row, jnp.where(sub > p, new, old))
                groups[v] = new
    return groups


def factor_body(scale, gram_ref, r_ref, own_ref, other_ref, work, roots):
    narrow = gram_ref.shape[2]
    rows = narrow // 2
    snap = lax.axis_index("snap")
    row = lax.broadcasted_iota(jnp.int32, (narrow, narrow), 0)
    col = lax.broadcasted_iota(jnp.int32, (narrow, narrow), 1)

    def gram(i):
        here = slice(i * rows, (i + 1) * rows)
        return jnp.concatenate([gram_ref[0, here, :], gram_ref[1, here, :]], axis=0)

    def dot(a, b, dims):
        return lax.dot_general(
            a, b, (dims, ((), ())), precision=HIGH, preferred_element_type=jnp.float32
        )

    def diagonal(which):
        full = work[which]
        inverse = jnp.where(col <= row, full, 0.0)
        upper = jnp.where(col > row, full, 0.0)
        upper = jnp.where(col == row, 1.0 / full, upper)
        return inverse, upper

    work[0] = gram(0)
    work[1] = gram(1)

    @pl.loop(0, 2)
    def _(block):
        groups = [
            work[block, SUBLANES * v:SUBLANES * (v + 1), :] for v in range(narrow // SUBLANES)
        ]
        for v, group in enumerate(eliminate(groups)):
            work[block, SUBLANES * v:SUBLANES * (v + 1), :] = group

        @pl.when(block == 0)
        def _():
            inverse, _ = diagonal(0)
            right = dot(inverse, gram(2), ((1,), (0,)))
            roots[...] = right
            work[1] = work[1] - dot(right, right, ((0,), (0,)))

    inverse0, upper0 = diagonal(0)
    inverse1, upper1 = diagonal(1)
    right = roots[...]
    below = -dot(inverse1, dot(right, inverse0, ((0,), (0,))), ((1,), (0,)))
    r_ref[0:narrow, 0:narrow] = upper0 / scale
    r_ref[0:narrow, narrow:] = right / scale
    r_ref[narrow:, 0:narrow] = jnp.zeros_like(right)
    r_ref[narrow:, narrow:] = upper1 / scale
    own = jnp.where(snap == 0, inverse0, inverse1)
    own_ref[...] = (own * scale).astype(own_ref.dtype)
    other = jnp.where(snap == 0, 0.0, below)
    other_ref[...] = (other * scale).astype(other_ref.dtype)


def meet(sem, stage, chip_row, core):
    y, z = lax.rem(chip_row, 2), lax.div(chip_row, 2)
    last = lax.axis_size("row") // 4 - 1

    def signal(chip):
        pl.semaphore_signal(
            sem.at[stage], inc=1, device_id={"row": 2 * chip + core}, device_id_type=MESH
        )

    signal(chip_row + 1 - 2 * y)

    @pl.when(z > 0)
    def _():
        signal(chip_row - 2)

    @pl.when(z < last)
    def _():
        signal(chip_row + 2)


def meetings(chip_row):
    z = lax.div(chip_row, 2)
    last = lax.axis_size("row") // 4 - 1
    return 1 + jnp.where(z > 0, 1, 0) + jnp.where(z < last, 1, 0)


def panel_kernel(
    units, mid, per, room, scale, counts_ref, x_ref,
    own_low, own_top, got, top, r_ref, own_w_ref, other_w_ref, load_ref,
    mine, near, summed, theirs, part, parts, gram_ref, work, roots,
    tally, tally_s, loose, packed, back,
    load_sem, send_sem, recv_sem, met, near_send, near_recv, sum_send, sum_recv,
    part_send, part_recv, out_send, out_recv, tally_send, tally_recv, tally_copy,
    loose_send, loose_recv, loose_copy, pack_send, pack_recv, back_send, back_recv,
):
    snap = lax.axis_index("snap")
    me = lax.axis_index("row")
    n = lax.axis_size("row")
    core, chip = lax.rem(me, 2), lax.div(me, 2)
    chips = n // 2
    other = {"snap": 1 - snap}
    pair = {"row": me + 1 - 2 * core}
    narrow, slots = x_ref.shape
    step = slots // units
    base = got.shape[1]
    low = base // step
    count = counts_ref[0]
    rows = narrow // 2
    y, z = lax.rem(chip, 2), lax.div(chip, 2)
    last = chips // 2 - 1

    barrier = pltpu.get_barrier_semaphore()

    def greet(device):
        pl.semaphore_signal(barrier, inc=1, device_id=device, device_id_type=MESH)

    greet(other)
    greet(pair)
    greet({"row": 2 * (chip + 1 - 2 * y) + core})

    @pl.when(z > 0)
    def _():
        greet({"row": me - 4})

    @pl.when(z < last)
    def _():
        greet({"row": me + 4})

    tally[me] = jnp.full(tally.shape[1:], count, jnp.int32)
    wide = 8
    span = slots // wide
    loads = []
    for c in range(wide):
        at = pl.ds(c * span, span)
        into, start = (own_low, c * span) if c * span < base else (own_top, c * span - base)
        copy = pltpu.make_async_copy(
            x_ref.at[:, at], into.at[:, pl.ds(start, span)], load_sem.at[c]
        )
        copy.start()
        loads.append(copy)

    pl.semaphore_wait(barrier, 2 + meetings(chip))

    def bulk(u):
        into, start = (got, u * step) if u < low else (top, (u - low) * step)
        return pltpu.make_async_remote_copy(
            src_ref=x_ref.at[:, pl.ds(u * step, step)], dst_ref=into.at[:, pl.ds(start, step)],
            send_sem=send_sem.at[u], recv_sem=recv_sem.at[u],
            device_id=other, device_id_type=MESH,
        )

    def arrived(u):
        if u < low:
            return got[:, u * step:(u + 1) * step]
        return top[:, (u - low) * step:(u - low + 1) * step]

    def send(which, first, stop):
        @pl.when(snap == which)
        def _():
            for u in range(first, stop):
                bulk(u).start()

    ahead = 6
    behind = ahead + 5
    send(0, 0, ahead)
    send(1, mid, mid + ahead)

    for stage in range(met.shape[0]):
        meet(met, stage, chip, core)
        pl.semaphore_wait(met.at[stage], meetings(chip))

    def tally_to(d):
        return pltpu.make_async_remote_copy(
            src_ref=tally.at[me], dst_ref=tally.at[me],
            send_sem=tally_send.at[d - 1], recv_sem=tally_recv.at[d - 1],
            device_id={"row": lax.rem(me + d, n)}, device_id_type=MESH,
        )

    for d in range(1, n):
        tally_to(d).start()

    def loose_to(d, q):
        at = (d - 1) * per + q
        return pltpu.make_async_remote_copy(
            src_ref=x_ref.at[:, pl.ds(base + LANES * (d + n * q), LANES)],
            dst_ref=loose.at[me + n * q],
            send_sem=loose_send.at[at], recv_sem=loose_recv.at[at],
            device_id={"row": lax.rem(me + d, n)}, device_id_type=MESH,
        )

    def loose_own(q):
        return pltpu.make_async_copy(
            x_ref.at[:, pl.ds(base + LANES * n * q, LANES)], loose.at[me + n * q],
            loose_copy.at[q],
        )

    hops = [(d, q) for q in range(per) for d in range(1, n)]

    @pl.when(snap == 0)
    def _():
        for d, q in hops:
            loose_to(d, q).start()
        for q in range(per):
            loose_own(q).start()

    def masked(block, start):
        lane = lax.broadcasted_iota(jnp.int32, block.shape, 1) + start
        return jnp.where(lane < count, block, jnp.zeros_like(block))

    def owned(start, size):
        if start < base:
            return own_low[:, start:start + size]
        return own_top[:, start - base:start - base + size]

    total = jnp.zeros((narrow, narrow), jnp.float32)
    for c in range(wide):
        loads[c].wait()
        block = owned(c * span, span)
        total = total + mxu_nt(masked(block, c * span), block)
    mine[0] = total

    def sum_copy(i):
        away = pltpu.make_async_remote_copy(
            src_ref=mine.at[i, pl.ds(pl.multiple_of((1 - core) * rows, SUBLANES), rows)],
            dst_ref=near.at[i],
            send_sem=near_send.at[i], recv_sem=near_recv.at[i],
            device_id=pair, device_id_type=MESH,
        )
        away.start()
        away.wait()
        kept = mine[i, pl.ds(pl.multiple_of(core * rows, SUBLANES), rows), :]
        summed[i] = kept + near[i]
        return pltpu.make_async_remote_copy(
            src_ref=summed.at[i], dst_ref=theirs.at[i],
            send_sem=sum_send.at[i], recv_sem=sum_recv.at[i],
            device_id=other, device_id_type=MESH,
        )

    diagonal = sum_copy(0)
    diagonal.start()
    send(0, ahead, behind)
    send(1, mid + ahead, units)
    mine[1] = jnp.zeros((narrow, narrow), jnp.float32)

    def cross(first, stop):
        for u in range(first, stop):
            bulk(u).wait_recv()
            block = masked(owned(u * step, step), u * step)

            @pl.when(snap == 1)
            def _():
                mine[1] = mine[1] + mxu_nt(arrived(u), block)

            @pl.when(snap == 0)
            def _():
                mine[1] = mine[1] + mxu_nt(block, arrived(u))

    def learn():
        for d in range(1, n):
            tally_to(d).wait_recv()
        copy = pltpu.make_async_copy(tally, tally_s, tally_copy)
        copy.start()
        copy.wait()
        seen, before = jnp.int32(0), []
        for q in range(per):
            for i in range(n):
                rel = lax.rem(me - i + n, n)
                live = (base + LANES * (rel + n * q) < tally_s[i, 0, 0]).astype(jnp.int32)
                before.append(seen)
                seen = seen + live
        return before, before[1:] + [seen]

    def pack_to(h):
        size = (room // 2, room - room // 2)[h]
        at = pl.ds(h * (room // 2), size)
        return pltpu.make_async_remote_copy(
            src_ref=packed.at[0, at], dst_ref=packed.at[1, at],
            send_sem=pack_send.at[h], recv_sem=pack_recv.at[h],
            device_id=other, device_id_type=MESH,
        )

    def back_to(d, q):
        at = (d - 1) * per + q
        home = lax.rem(me + n - d, n)
        return pltpu.make_async_remote_copy(
            src_ref=back.at[home + n * q],
            dst_ref=top.at[:, pl.ds(LANES * (d + n * q), LANES)],
            send_sem=back_send.at[at], recv_sem=back_recv.at[at],
            device_id={"row": home}, device_id_type=MESH,
        )

    @pl.when(snap == 0)
    def _():
        cross(mid, mid + 9)
        _, after = learn()
        for q in range(per):
            loose_own(q).wait()
        for d, q in hops:
            loose_to(d, q).wait_recv()
        for p in range(room):
            pick = jnp.int32(0)
            for passed in after:
                pick = pick + (passed <= p).astype(jnp.int32)
            pick = jnp.minimum(pick, per * n - 1)
            packed[0, p] = loose[pick]
        for h in range(2):
            pack_to(h).start()
        for u in range(behind, mid + 1):
            bulk(u).start()
        cross(mid + 9, units)

    split = len(hops) // 2

    @pl.when(snap == 1)
    def _():
        cross(0, behind)
        before, _ = learn()
        for h in range(2):
            pack_to(h).wait_recv()
        for f, place in enumerate(before):
            place = jnp.minimum(place, room - 1)
            back[f] = packed[1, place]
        for d, q in hops[:split]:
            back_to(d, q).start()
        for q in range(per):
            top[:, LANES * n * q:LANES * (n * q + 1)] = back[me + n * q]
        cross(behind, mid)

    crossed = sum_copy(1)
    crossed.start()
    send(0, mid + 1, low)

    diagonal.wait()
    part[0:rows, :] = jnp.where(snap == 0, summed[0], theirs[0])
    part[rows:2 * rows, :] = jnp.where(snap == 0, theirs[0], summed[0])
    crossed.wait()
    part[2 * rows:3 * rows, :] = summed[1] + theirs[1]

    lines = part.shape[0] // chips

    def at(i):
        return pl.ds(pl.multiple_of(i * lines, SUBLANES), lines)

    copies = []
    for d in range(1, chips):
        peer = lax.rem(chip + d, chips)
        copy = pltpu.make_async_remote_copy(
            src_ref=part.at[at(peer)], dst_ref=parts.at[d - 1],
            send_sem=part_send.at[d - 1], recv_sem=part_recv.at[d - 1],
            device_id={"row": 2 * peer + core}, device_id_type=MESH,
        )
        copy.start()
        copies.append(copy)
    total = part[at(chip), :]
    for d in range(1, chips):
        copies[d - 1].wait_recv()
        total = total + parts[d - 1]
    gram_ref[core, at(chip), :] = total
    results = []
    for d in range(1, n):
        peer = lax.rem(me + d, n)
        copy = pltpu.make_async_remote_copy(
            src_ref=gram_ref.at[core, at(chip)], dst_ref=gram_ref.at[core, at(chip)],
            send_sem=out_send.at[d - 1], recv_sem=out_recv.at[d - 1],
            device_id={"row": peer}, device_id_type=MESH,
        )
        copy.start()
        results.append(copy)

    @pl.when(snap == 1)
    def _():
        for d, q in hops[split:]:
            back_to(d, q).start()

    for copy in copies:
        copy.wait_send()
    for copy in results:
        copy.wait()

    factor_body(scale, gram_ref, r_ref, own_w_ref, other_w_ref, work, roots)

    lane = lax.broadcasted_iota(jnp.int32, tally.shape[1:], 1)
    full = jnp.zeros(tally.shape[1:], jnp.int32)
    for i in range(n):
        rel = jnp.where(lane >= i, lane - i, lane - i + n)
        for q in range(per):
            full = full + jnp.where(base + LANES * (rel + n * q) < tally[i], 1, 0)
    full = jnp.where(lane < n, full, 0).astype(jnp.float32)
    load_ref[0, 0] = jnp.max(full)

    for d in range(1, n):
        tally_to(d).wait_send()

    @pl.when(snap == 0)
    def _():
        for h in range(2):
            pack_to(h).wait_send()
        for d, q in hops:
            loose_to(d, q).wait_send()
        for u in range(low):
            bulk(u).wait_send()

    @pl.when(snap == 1)
    def _():
        for u in range(mid, units):
            bulk(u).wait_send()
        for d, q in hops:
            back_to(d, q).wait()
        for u in range(mid, low):
            bulk(u).wait_recv()


def exchange_and_factor(snapshots, counts, scale, room, per, units=32):
    narrow, slots = snapshots.shape
    dtype = snapshots.dtype
    n = lax.axis_size("row")
    chips = n // 2
    rows = narrow // 2
    height = 3 * rows
    tail = per * n * LANES
    f32 = jnp.float32
    vmem = pl.BlockSpec(memory_space=pltpu.VMEM)
    smem = pl.BlockSpec(memory_space=pltpu.SMEM)
    dma = pltpu.SemaphoreType.DMA
    return pl.pallas_call(
        functools.partial(panel_kernel, units, 14, per, room, scale),
        name="exchange_and_factor",
        out_shape=(
            jax.ShapeDtypeStruct((narrow, slots - tail), dtype),
            jax.ShapeDtypeStruct((narrow, tail), dtype),
            jax.ShapeDtypeStruct((narrow, slots - tail), dtype),
            jax.ShapeDtypeStruct((narrow, tail), dtype),
            jax.ShapeDtypeStruct((2 * narrow, 2 * narrow), f32),
            jax.ShapeDtypeStruct((narrow, narrow), dtype),
            jax.ShapeDtypeStruct((narrow, narrow), dtype),
            jax.ShapeDtypeStruct((1, 1), f32),
        ),
        in_specs=[smem, pl.BlockSpec(memory_space=pltpu.HBM)],
        out_specs=(vmem, vmem, vmem, vmem, vmem, vmem, vmem, smem),
        scratch_shapes=[
            pltpu.VMEM((2, narrow, narrow), f32),
            pltpu.VMEM((2, rows, narrow), f32),
            pltpu.VMEM((2, rows, narrow), f32),
            pltpu.VMEM((2, rows, narrow), f32),
            pltpu.VMEM((height, narrow), f32),
            pltpu.VMEM((chips - 1, height // chips, narrow), f32),
            pltpu.VMEM((2, height, narrow), f32),
            pltpu.VMEM((2, narrow, narrow), f32),
            pltpu.VMEM((narrow, narrow), f32),
            pltpu.VMEM((n, 1, LANES), jnp.int32),
            pltpu.SMEM((n, 1, LANES), jnp.int32),
            pltpu.VMEM((per * n, narrow, LANES), dtype),
            pltpu.VMEM((2, room, narrow, LANES), dtype),
            pltpu.VMEM((per * n, narrow, LANES), dtype),
            dma((8,)),
            dma((units,)),
            dma((units,)),
            pltpu.SemaphoreType.REGULAR((4,)),
            dma((2,)),
            dma((2,)),
            dma((2,)),
            dma((2,)),
            dma((chips - 1,)),
            dma((chips - 1,)),
            dma((n - 1,)),
            dma((n - 1,)),
            dma((n - 1,)),
            dma((n - 1,)),
            dma,
            dma((per * (n - 1),)),
            dma((per * (n - 1),)),
            dma((per,)),
            dma((2,)),
            dma((2,)),
            dma((per * (n - 1),)),
            dma((per * (n - 1),)),
        ],
        compiler_params=pltpu.CompilerParams(
            collective_id=0, has_side_effects=True, vmem_limit_bytes=44 << 20
        ),
    )(counts, snapshots)


def resend_kernel(x_ref, top_ref, send_sem, recv_sem):
    snap = lax.axis_index("snap")
    other = {"snap": 1 - snap}
    start = x_ref.shape[1] - top_ref.shape[1]
    barrier = pltpu.get_barrier_semaphore()
    pl.semaphore_signal(barrier, inc=1, device_id=other, device_id_type=MESH)
    pl.semaphore_wait(barrier, 1)
    copy = pltpu.make_async_remote_copy(
        src_ref=x_ref.at[:, pl.ds(start, top_ref.shape[1])], dst_ref=top_ref,
        send_sem=send_sem, recv_sem=recv_sem, device_id=other, device_id_type=MESH,
    )
    copy.start()
    copy.wait()


def resend(snapshots, tail):
    return pl.pallas_call(
        resend_kernel,
        name="resend",
        out_shape=jax.ShapeDtypeStruct((snapshots.shape[0], tail), snapshots.dtype),
        in_specs=[pl.BlockSpec(memory_space=pl.ANY)],
        out_specs=pl.BlockSpec(memory_space=pl.ANY),
        scratch_shapes=[pltpu.SemaphoreType.DMA, pltpu.SemaphoreType.DMA],
        compiler_params=pltpu.CompilerParams(collective_id=1, has_side_effects=True),
    )(snapshots)


def basis_kernel(first, pieces, counts_ref, own_w, other_w, own_ref, got_ref, *rest):
    if first == 0:
        r_in, load_in, out_ref, r_out, load_out, stage, sems = rest
        load_out[0, 0] = load_in[0, 0]
    else:
        _, out_ref, stage, sems = rest
    snap = lax.axis_index("snap")
    step = own_ref.shape[1] // pieces
    count = counts_ref[0]

    def piece(c):
        return pltpu.make_async_copy(
            stage.at[:, pl.ds(c * step, step)], out_ref.at[:, pl.ds(first + c * step, step)],
            sems.at[c],
        )

    def form(weights, block, c):
        value = lax.dot_general(
            weights, block, (((1,), (0,)), ((), ())), preferred_element_type=jnp.float32
        )
        lane = lax.broadcasted_iota(jnp.int32, value.shape, 1) + first + c * step
        value = jnp.where(lane < count, value, 0.0).astype(stage.dtype)
        stage[:, c * step:(c + 1) * step] = value
        piece(c).start()

    @pl.when(snap == 0)
    def _():
        weights = own_w[...]
        for c in range(pieces):
            form(weights, own_ref[:, c * step:(c + 1) * step], c)

    @pl.when(snap == 1)
    def _():
        weights = jnp.concatenate([own_w[...], other_w[...]], axis=1)
        for c in range(pieces):
            here = slice(c * step, (c + 1) * step)
            form(weights, jnp.concatenate([own_ref[:, here], got_ref[:, here]], axis=0), c)

    if first == 0:
        r_out[...] = r_in[...]
    for c in range(pieces):
        piece(c).wait()


def form_basis(counts, own_w, other_w, own, got, first, slots, *more, step=2048):
    narrow, width = own.shape
    pieces = width // step
    vmem = pl.BlockSpec(memory_space=pltpu.VMEM)
    smem = pl.BlockSpec(memory_space=pltpu.SMEM)
    hbm = pl.BlockSpec(memory_space=pltpu.HBM)
    out_shape = [jax.ShapeDtypeStruct((narrow, slots), own.dtype)]
    out_specs = [hbm]
    if first == 0:
        out_shape += [jax.ShapeDtypeStruct(m.shape, m.dtype) for m in more]
        out_specs += [vmem, smem]
        more_specs = [vmem, smem]
    else:
        more_specs = [hbm]
    return pl.pallas_call(
        functools.partial(basis_kernel, first, pieces),
        name="form_basis",
        out_shape=out_shape,
        in_specs=[smem, vmem, vmem, vmem, vmem, *more_specs],
        out_specs=out_specs,
        input_output_aliases={5: 0} if first else {},
        scratch_shapes=[
            pltpu.VMEM((narrow, width), own.dtype),
            pltpu.SemaphoreType.DMA((pieces,)),
        ],
        compiler_params=pltpu.CompilerParams(vmem_limit_bytes=16 << 20),
        cost_estimate=pl.CostEstimate(
            flops=4 * narrow * narrow * width, bytes_accessed=8 * narrow * width, transcendentals=0
        ),
    )(counts, own_w, other_w, own, got, *more)


def halves(snapshots, counts, room=17, per=2):
    slots = snapshots.shape[1]
    scale = math.sqrt(slots * lax.axis_size("row"))
    own, own_top, got, top, r_factor, own_w, other_w, load = exchange_and_factor(
        snapshots, counts, scale, room, per
    )
    form = functools.partial(form_basis, counts, own_w, other_w)
    basis, r_factor, load = form(own, got, 0, slots, r_factor, load)
    top = lax.cond(
        load[0, 0] > room, lambda kept: resend(snapshots, kept.shape[1]), lambda kept: kept, top
    )
    (basis,) = form(own_top, top, own.shape[1], slots, basis)
    return (basis, r_factor)


def two_halves(mesh):
    return mesh.shape["snap"] == 2 and mesh.shape["row"] == 16


def solution(mesh):
    placed = (P("snap", "row"), P("row"))
    body = halves if two_halves(mesh) else shards
    return jax.shard_map(
        body, mesh=mesh, in_specs=placed, out_specs=(P("snap", "row"), P()), check_vma=False
    )
```

```python
import functools
import math

import jax
import jax.numpy as jnp
from jax import lax
from jax.experimental import pallas as pl
from jax.experimental.pallas import tpu as pltpu
from jax.sharding import PartitionSpec as P

MESH = pl.DeviceIdType.MESH
HIGH = lax.Precision.HIGHEST
LANES = 128
SUBLANES = 8


def gram_of(block):
    return lax.dot_general(
        block, block, (((1,), (1,)), ((), ())), preferred_element_type=jnp.float32
    )


def factors(gram, scale):
    lower = jnp.linalg.cholesky(gram)
    r_factor = lower.T / scale
    width = gram.shape[0]
    inverse = lax.linalg.triangular_solve(
        lower, jnp.eye(width, dtype=jnp.float32), left_side=True, lower=True
    ).T
    weights = (inverse * scale).astype(jnp.bfloat16)
    return (r_factor, weights)


def apply_weights(weights, block):
    return lax.dot_general(
        weights, block, (((0,), (0,)), ((), ())), preferred_element_type=jnp.float32
    ).astype(jnp.bfloat16)


def shards(snapshots, counts):
    narrow, slots = snapshots.shape
    slot = lax.broadcasted_iota(jnp.int32, (1, slots), 1)
    live = jnp.where(slot < counts[0], snapshots, jnp.zeros_like(snapshots))
    scale = math.sqrt(slots * lax.axis_size("row"))
    whole = lax.all_gather(live, "snap", axis=0, tiled=True)
    gram = lax.psum(gram_of(whole), "row")
    r_factor, weights = factors(gram, scale)
    start = lax.axis_index("snap") * narrow
    own_weights = lax.dynamic_slice_in_dim(weights, start, narrow, 1)
    basis = apply_weights(own_weights, whole)
    return (basis, r_factor)


def mxu_nt(a, b):
    return lax.dot_general(
        a, b, (((1,), (1,)), ((), ())), preferred_element_type=jnp.float32
    )


def eliminate(groups):
    shape = groups[0].shape
    tall = shape[0]
    lane = lax.broadcasted_iota(jnp.int32, shape, 1)
    sub = lax.broadcasted_iota(jnp.int32, shape, 0)
    groups = list(groups)
    count = len(groups)

    def line(block, p):
        return jnp.broadcast_to(block[p:p + 1, :], shape)

    for g in range(count):
        columns = [
            [
                jnp.broadcast_to(groups[v][:, g * tall + q:g * tall + q + 1], shape)
                for v in range(g, count)
            ]
            for q in range(tall)
        ]
        for p in range(tall):
            here = lane == g * tall + p
            pivot = line(columns[p][0], p)
            root = lax.rsqrt(pivot)
            root = root * (1.5 - 0.5 * pivot * root * root)
            lefts = [column * root for column in columns[p]]
            lefts[0] = jnp.where(sub > p, lefts[0], 0.0)
            for q in range(p + 1, tall):
                top = line(columns[q][0], p) * root
                columns[q] = [c - m * top for c, m in zip(columns[q], lefts)]
            row = jnp.where(here, root, line(groups[g], p) * root)
            for v in range(g, count):
                old = groups[v]
                new = jnp.where(here, 0.0, old) - lefts[v - g] * row
                if v == g:
                    new = jnp.where(sub == p, row, jnp.where(sub > p, new, old))
                groups[v] = new
    return groups


def factor_body(scale, gram_ref, r_ref, own_ref, other_ref, work, roots):
    narrow = gram_ref.shape[2]
    rows = narrow // 2
    snap = lax.axis_index("snap")
    row = lax.broadcasted_iota(jnp.int32, (narrow, narrow), 0)
    col = lax.broadcasted_iota(jnp.int32, (narrow, narrow), 1)

    def gram(i):
        here = slice(i * rows, (i + 1) * rows)
        return jnp.concatenate([gram_ref[0, here, :], gram_ref[1, here, :]], axis=0)

    def dot(a, b, dims):
        return lax.dot_general(
            a, b, (dims, ((), ())), precision=HIGH, preferred_element_type=jnp.float32
        )

    def diagonal(which):
        full = work[which]
        inverse = jnp.where(col <= row, full, 0.0)
        upper = jnp.where(col > row, full, 0.0)
        upper = jnp.where(col == row, 1.0 / full, upper)
        return inverse, upper

    work[0] = gram(0)
    work[1] = gram(1)

    @pl.loop(0, 2)
    def _(block):
        groups = [
            work[block, SUBLANES * v:SUBLANES * (v + 1), :] for v in range(narrow // SUBLANES)
        ]
        for v, group in enumerate(eliminate(groups)):
            work[block, SUBLANES * v:SUBLANES * (v + 1), :] = group

        @pl.when(block == 0)
        def _():
            inverse, _ = diagonal(0)
            right = dot(inverse, gram(2), ((1,), (0,)))
            roots[...] = right
            work[1] = work[1] - dot(right, right, ((0,), (0,)))

    inverse0, upper0 = diagonal(0)
    inverse1, upper1 = diagonal(1)
    right = roots[...]
    below = -dot(inverse1, dot(right, inverse0, ((0,), (0,))), ((1,), (0,)))
    r_ref[0:narrow, 0:narrow] = upper0 / scale
    r_ref[0:narrow, narrow:] = right / scale
    r_ref[narrow:, 0:narrow] = jnp.zeros_like(right)
    r_ref[narrow:, narrow:] = upper1 / scale
    own = jnp.where(snap == 0, inverse0, inverse1)
    own_ref[...] = (own * scale).astype(own_ref.dtype)
    other = jnp.where(snap == 0, 0.0, below)
    other_ref[...] = (other * scale).astype(other_ref.dtype)


def meet(sem, stage, chip_row, core):
    y, z = lax.rem(chip_row, 2), lax.div(chip_row, 2)
    last = lax.axis_size("row") // 4 - 1

    def signal(chip):
        pl.semaphore_signal(
            sem.at[stage], inc=1, device_id={"row": 2 * chip + core}, device_id_type=MESH
        )

    signal(chip_row + 1 - 2 * y)

    @pl.when(z > 0)
    def _():
        signal(chip_row - 2)

    @pl.when(z < last)
    def _():
        signal(chip_row + 2)


def meetings(chip_row):
    z = lax.div(chip_row, 2)
    last = lax.axis_size("row") // 4 - 1
    return 1 + jnp.where(z > 0, 1, 0) + jnp.where(z < last, 1, 0)


def panel_kernel(
    units, mid, per, room, scale, counts_ref, x_ref,
    own_low, own_top, got, top, r_ref, own_w_ref, other_w_ref, load_ref,
    mine, near, summed, theirs, part, parts, gram_ref, work, roots,
    tally, tally_s, loose, packed, back,
    load_sem, send_sem, recv_sem, met, near_send, near_recv, sum_send, sum_recv,
    part_send, part_recv, out_send, out_recv, tally_send, tally_recv, tally_copy,
    loose_send, loose_recv, loose_copy, pack_send, pack_recv, back_send, back_recv,
):
    snap = lax.axis_index("snap")
    me = lax.axis_index("row")
    n = lax.axis_size("row")
    core, chip = lax.rem(me, 2), lax.div(me, 2)
    chips = n // 2
    other = {"snap": 1 - snap}
    pair = {"row": me + 1 - 2 * core}
    narrow, slots = x_ref.shape
    step = slots // units
    base = got.shape[1]
    low = base // step
    count = counts_ref[0]
    rows = narrow // 2
    y, z = lax.rem(chip, 2), lax.div(chip, 2)
    last = chips // 2 - 1

    barrier = pltpu.get_barrier_semaphore()

    def greet(device):
        pl.semaphore_signal(barrier, inc=1, device_id=device, device_id_type=MESH)

    greet(other)
    greet(pair)
    greet({"row": 2 * (chip + 1 - 2 * y) + core})

    @pl.when(z > 0)
    def _():
        greet({"row": me - 4})

    @pl.when(z < last)
    def _():
        greet({"row": me + 4})

    tally[me] = jnp.full(tally.shape[1:], count, jnp.int32)
    wide = 8
    span = slots // wide
    loads = []
    for c in range(wide):
        at = pl.ds(c * span, span)
        into, start = (own_low, c * span) if c * span < base else (own_top, c * span - base)
        copy = pltpu.make_async_copy(
            x_ref.at[:, at], into.at[:, pl.ds(start, span)], load_sem.at[c]
        )
        copy.start()
        loads.append(copy)

    pl.semaphore_wait(barrier, 2 + meetings(chip))

    def bulk(u):
        into, start = (got, u * step) if u < low else (top, (u - low) * step)
        return pltpu.make_async_remote_copy(
            src_ref=x_ref.at[:, pl.ds(u * step, step)], dst_ref=into.at[:, pl.ds(start, step)],
            send_sem=send_sem.at[u], recv_sem=recv_sem.at[u],
            device_id=other, device_id_type=MESH,
        )

    def arrived(u):
        if u < low:
            return got[:, u * step:(u + 1) * step]
        return top[:, (u - low) * step:(u - low + 1) * step]

    def send(which, first, stop):
        @pl.when(snap == which)
        def _():
            for u in range(first, stop):
                bulk(u).start()

    ahead = 6
    behind = ahead + 5
    send(0, 0, ahead)
    send(1, mid, mid + ahead)

    for stage in range(met.shape[0]):
        meet(met, stage, chip, core)
        pl.semaphore_wait(met.at[stage], meetings(chip))

    def tally_to(d):
        return pltpu.make_async_remote_copy(
            src_ref=tally.at[me], dst_ref=tally.at[me],
            send_sem=tally_send.at[d - 1], recv_sem=tally_recv.at[d - 1],
            device_id={"row": lax.rem(me + d, n)}, device_id_type=MESH,
        )

    for d in range(1, n):
        tally_to(d).start()

    def loose_to(d, q):
        at = (d - 1) * per + q
        return pltpu.make_async_remote_copy(
            src_ref=x_ref.at[:, pl.ds(base + LANES * (d + n * q), LANES)],
            dst_ref=loose.at[me + n * q],
            send_sem=loose_send.at[at], recv_sem=loose_recv.at[at],
            device_id={"row": lax.rem(me + d, n)}, device_id_type=MESH,
        )

    def loose_own(q):
        return pltpu.make_async_copy(
            x_ref.at[:, pl.ds(base + LANES * n * q, LANES)], loose.at[me + n * q],
            loose_copy.at[q],
        )

    hops = [(d, q) for q in range(per) for d in range(1, n)]

    @pl.when(snap == 0)
    def _():
        for d, q in hops:
            loose_to(d, q).start()
        for q in range(per):
            loose_own(q).start()

    def masked(block, start):
        lane = lax.broadcasted_iota(jnp.int32, block.shape, 1) + start
        return jnp.where(lane < count, block, jnp.zeros_like(block))

    def owned(start, size):
        if start < base:
            return own_low[:, start:start + size]
        return own_top[:, start - base:start - base + size]

    total = jnp.zeros((narrow, narrow), jnp.float32)
    for c in range(wide):
        loads[c].wait()
        block = owned(c * span, span)
        total = total + mxu_nt(masked(block, c * span), block)
    mine[0] = total

    def sum_copy(i):
        away = pltpu.make_async_remote_copy(
            src_ref=mine.at[i, pl.ds(pl.multiple_of((1 - core) * rows, SUBLANES), rows)],
            dst_ref=near.at[i],
            send_sem=near_send.at[i], recv_sem=near_recv.at[i],
            device_id=pair, device_id_type=MESH,
        )
        away.start()
        away.wait()
        kept = mine[i, pl.ds(pl.multiple_of(core * rows, SUBLANES), rows), :]
        summed[i] = kept + near[i]
        return pltpu.make_async_remote_copy(
            src_ref=summed.at[i], dst_ref=theirs.at[i],
            send_sem=sum_send.at[i], recv_sem=sum_recv.at[i],
            device_id=other, device_id_type=MESH,
        )

    diagonal = sum_copy(0)
    diagonal.start()
    send(0, ahead, behind)
    send(1, mid + ahead, units)
    mine[1] = jnp.zeros((narrow, narrow), jnp.float32)

    def cross(first, stop):
        for u in range(first, stop):
            bulk(u).wait_recv()
            block = masked(owned(u * step, step), u * step)

            @pl.when(snap == 1)
            def _():
                mine[1] = mine[1] + mxu_nt(arrived(u), block)

            @pl.when(snap == 0)
            def _():
                mine[1] = mine[1] + mxu_nt(block, arrived(u))

    def learn():
        for d in range(1, n):
            tally_to(d).wait_recv()
        copy = pltpu.make_async_copy(tally, tally_s, tally_copy)
        copy.start()
        copy.wait()
        seen, before = jnp.int32(0), []
        for q in range(per):
            for i in range(n):
                rel = lax.rem(me - i + n, n)
                live = (base + LANES * (rel + n * q) < tally_s[i, 0, 0]).astype(jnp.int32)
                before.append(seen)
                seen = seen + live
        return before, before[1:] + [seen]

    def note_load():
        lane = lax.broadcasted_iota(jnp.int32, tally.shape[1:], 1)
        full = jnp.zeros(tally.shape[1:], jnp.int32)
        for i in range(n):
            rel = jnp.where(lane >= i, lane - i, lane - i + n)
            for q in range(per):
                full = full + jnp.where(base + LANES * (rel + n * q) < tally[i], 1, 0)
        full = jnp.where(lane < n, full, 0).astype(jnp.float32)
        load_ref[0, 0] = jnp.max(full)

    def pack_to(h):
        size = (room // 2, room - room // 2)[h]
        at = pl.ds(h * (room // 2), size)
        return pltpu.make_async_remote_copy(
            src_ref=packed.at[0, at], dst_ref=packed.at[1, at],
            send_sem=pack_send.at[h], recv_sem=pack_recv.at[h],
            device_id=other, device_id_type=MESH,
        )

    def back_to(d, q):
        at = (d - 1) * per + q
        home = lax.rem(me + n - d, n)
        return pltpu.make_async_remote_copy(
            src_ref=back.at[home + n * q],
            dst_ref=top.at[:, pl.ds(LANES * (d + n * q), LANES)],
            send_sem=back_send.at[at], recv_sem=back_recv.at[at],
            device_id={"row": home}, device_id_type=MESH,
        )

    @pl.when(snap == 0)
    def _():
        cross(mid, mid + 9)
        _, after = learn()
        for q in range(per):
            loose_own(q).wait()
        for d, q in hops:
            loose_to(d, q).wait_recv()
        for p in range(room):
            pick = jnp.int32(0)
            for passed in after:
                pick = pick + (passed <= p).astype(jnp.int32)
            pick = jnp.minimum(pick, per * n - 1)
            packed[0, p] = loose[pick]
        for h in range(2):
            pack_to(h).start()
        for u in range(behind, mid + 1):
            bulk(u).start()
        note_load()
        cross(mid + 9, units)

    split = len(hops) // 2

    @pl.when(snap == 1)
    def _():
        cross(0, 8)
        before, _ = learn()
        cross(8, behind)
        for h in range(2):
            pack_to(h).wait_recv()
        for f, place in enumerate(before):
            place = jnp.minimum(place, room - 1)
            back[f] = packed[1, place]
        for d, q in hops[:split]:
            back_to(d, q).start()
        for q in range(per):
            top[:, LANES * n * q:LANES * (n * q + 1)] = back[me + n * q]
        note_load()
        cross(behind, mid)

    crossed = sum_copy(1)
    crossed.start()
    send(0, mid + 1, low)

    diagonal.wait()
    part[0:rows, :] = jnp.where(snap == 0, summed[0], theirs[0])
    part[rows:2 * rows, :] = jnp.where(snap == 0, theirs[0], summed[0])
    crossed.wait()
    part[2 * rows:3 * rows, :] = summed[1] + theirs[1]

    lines = part.shape[0] // chips

    def at(i):
        return pl.ds(pl.multiple_of(i * lines, SUBLANES), lines)

    copies = []
    for d in range(1, chips):
        peer = lax.rem(chip + d, chips)
        copy = pltpu.make_async_remote_copy(
            src_ref=part.at[at(peer)], dst_ref=parts.at[d - 1],
            send_sem=part_send.at[d - 1], recv_sem=part_recv.at[d - 1],
            device_id={"row": 2 * peer + core}, device_id_type=MESH,
        )
        copy.start()
        copies.append(copy)
    total = part[at(chip), :]
    for d in range(1, chips):
        copies[d - 1].wait_recv()
        total = total + parts[d - 1]
    gram_ref[core, at(chip), :] = total
    results = []
    for d in range(1, n):
        peer = lax.rem(me + d, n)
        copy = pltpu.make_async_remote_copy(
            src_ref=gram_ref.at[core, at(chip)], dst_ref=gram_ref.at[core, at(chip)],
            send_sem=out_send.at[d - 1], recv_sem=out_recv.at[d - 1],
            device_id={"row": peer}, device_id_type=MESH,
        )
        copy.start()
        results.append(copy)

    for copy in copies:
        copy.wait_send()
    for copy in results:
        copy.wait()

    @pl.when(snap == 1)
    def _():
        for d, q in hops[split:]:
            back_to(d, q).start()

    factor_body(scale, gram_ref, r_ref, own_w_ref, other_w_ref, work, roots)

    for d in range(1, n):
        tally_to(d).wait_send()

    @pl.when(snap == 0)
    def _():
        for h in range(2):
            pack_to(h).wait_send()
        for d, q in hops:
            loose_to(d, q).wait_send()
        for u in range(low):
            bulk(u).wait_send()

    @pl.when(snap == 1)
    def _():
        for u in range(mid, units):
            bulk(u).wait_send()
        for d, q in hops:
            back_to(d, q).wait()
        for u in range(mid, low):
            bulk(u).wait_recv()


def exchange_and_factor(snapshots, counts, scale, room, per, units=32):
    narrow, slots = snapshots.shape
    dtype = snapshots.dtype
    n = lax.axis_size("row")
    chips = n // 2
    rows = narrow // 2
    height = 3 * rows
    tail = per * n * LANES
    f32 = jnp.float32
    vmem = pl.BlockSpec(memory_space=pltpu.VMEM)
    smem = pl.BlockSpec(memory_space=pltpu.SMEM)
    dma = pltpu.SemaphoreType.DMA
    return pl.pallas_call(
        functools.partial(panel_kernel, units, 14, per, room, scale),
        name="exchange_and_factor",
        out_shape=(
            jax.ShapeDtypeStruct((narrow, slots - tail), dtype),
            jax.ShapeDtypeStruct((narrow, tail), dtype),
            jax.ShapeDtypeStruct((narrow, slots - tail), dtype),
            jax.ShapeDtypeStruct((narrow, tail), dtype),
            jax.ShapeDtypeStruct((2 * narrow, 2 * narrow), f32),
            jax.ShapeDtypeStruct((narrow, narrow), dtype),
            jax.ShapeDtypeStruct((narrow, narrow), dtype),
            jax.ShapeDtypeStruct((1, 1), f32),
        ),
        in_specs=[smem, pl.BlockSpec(memory_space=pltpu.HBM)],
        out_specs=(vmem, vmem, vmem, vmem, vmem, vmem, vmem, smem),
        scratch_shapes=[
            pltpu.VMEM((2, narrow, narrow), f32),
            pltpu.VMEM((2, rows, narrow), f32),
            pltpu.VMEM((2, rows, narrow), f32),
            pltpu.VMEM((2, rows, narrow), f32),
            pltpu.VMEM((height, narrow), f32),
            pltpu.VMEM((chips - 1, height // chips, narrow), f32),
            pltpu.VMEM((2, height, narrow), f32),
            pltpu.VMEM((2, narrow, narrow), f32),
            pltpu.VMEM((narrow, narrow), f32),
            pltpu.VMEM((n, 1, LANES), jnp.int32),
            pltpu.SMEM((n, 1, LANES), jnp.int32),
            pltpu.VMEM((per * n, narrow, LANES), dtype),
            pltpu.VMEM((2, room, narrow, LANES), dtype),
            pltpu.VMEM((per * n, narrow, LANES), dtype),
            dma((8,)),
            dma((units,)),
            dma((units,)),
            pltpu.SemaphoreType.REGULAR((4,)),
            dma((2,)),
            dma((2,)),
            dma((2,)),
            dma((2,)),
            dma((chips - 1,)),
            dma((chips - 1,)),
            dma((n - 1,)),
            dma((n - 1,)),
            dma((n - 1,)),
            dma((n - 1,)),
            dma,
            dma((per * (n - 1),)),
            dma((per * (n - 1),)),
            dma((per,)),
            dma((2,)),
            dma((2,)),
            dma((per * (n - 1),)),
            dma((per * (n - 1),)),
        ],
        compiler_params=pltpu.CompilerParams(
            collective_id=0, has_side_effects=True, vmem_limit_bytes=44 << 20
        ),
    )(counts, snapshots)


def resend_kernel(x_ref, top_ref, send_sem, recv_sem):
    snap = lax.axis_index("snap")
    other = {"snap": 1 - snap}
    start = x_ref.shape[1] - top_ref.shape[1]
    barrier = pltpu.get_barrier_semaphore()
    pl.semaphore_signal(barrier, inc=1, device_id=other, device_id_type=MESH)
    pl.semaphore_wait(barrier, 1)
    copy = pltpu.make_async_remote_copy(
        src_ref=x_ref.at[:, pl.ds(start, top_ref.shape[1])], dst_ref=top_ref,
        send_sem=send_sem, recv_sem=recv_sem, device_id=other, device_id_type=MESH,
    )
    copy.start()
    copy.wait()


def resend(snapshots, tail):
    return pl.pallas_call(
        resend_kernel,
        name="resend",
        out_shape=jax.ShapeDtypeStruct((snapshots.shape[0], tail), snapshots.dtype),
        in_specs=[pl.BlockSpec(memory_space=pl.ANY)],
        out_specs=pl.BlockSpec(memory_space=pl.ANY),
        scratch_shapes=[pltpu.SemaphoreType.DMA, pltpu.SemaphoreType.DMA],
        compiler_params=pltpu.CompilerParams(collective_id=1, has_side_effects=True),
    )(snapshots)


def basis_kernel(first, pieces, counts_ref, own_w, other_w, own_ref, got_ref, *rest):
    if first == 0:
        r_in, load_in, out_ref, r_out, load_out, stage, sems = rest
        load_out[0, 0] = load_in[0, 0]
    else:
        _, out_ref, stage, sems = rest
    snap = lax.axis_index("snap")
    step = own_ref.shape[1] // pieces
    count = counts_ref[0]

    def piece(c):
        return pltpu.make_async_copy(
            stage.at[:, pl.ds(c * step, step)], out_ref.at[:, pl.ds(first + c * step, step)],
            sems.at[c],
        )

    def form(weights, block, c):
        value = lax.dot_general(
            weights, block, (((1,), (0,)), ((), ())), preferred_element_type=jnp.float32
        )
        lane = lax.broadcasted_iota(jnp.int32, value.shape, 1) + first + c * step
        value = jnp.where(lane < count, value, 0.0).astype(stage.dtype)
        stage[:, c * step:(c + 1) * step] = value
        piece(c).start()

    @pl.when(snap == 0)
    def _():
        weights = own_w[...]
        for c in range(pieces):
            form(weights, own_ref[:, c * step:(c + 1) * step], c)

    @pl.when(snap == 1)
    def _():
        weights = jnp.concatenate([own_w[...], other_w[...]], axis=1)
        for c in range(pieces):
            here = slice(c * step, (c + 1) * step)
            form(weights, jnp.concatenate([own_ref[:, here], got_ref[:, here]], axis=0), c)

    if first == 0:
        r_out[...] = r_in[...]
    for c in range(pieces):
        piece(c).wait()


def form_basis(counts, own_w, other_w, own, got, first, slots, *more, step=2048):
    narrow, width = own.shape
    pieces = width // step
    vmem = pl.BlockSpec(memory_space=pltpu.VMEM)
    smem = pl.BlockSpec(memory_space=pltpu.SMEM)
    hbm = pl.BlockSpec(memory_space=pltpu.HBM)
    out_shape = [jax.ShapeDtypeStruct((narrow, slots), own.dtype)]
    out_specs = [hbm]
    if first == 0:
        out_shape += [jax.ShapeDtypeStruct(m.shape, m.dtype) for m in more]
        out_specs += [vmem, smem]
        more_specs = [vmem, smem]
    else:
        more_specs = [hbm]
    return pl.pallas_call(
        functools.partial(basis_kernel, first, pieces),
        name="form_basis",
        out_shape=out_shape,
        in_specs=[smem, vmem, vmem, vmem, vmem, *more_specs],
        out_specs=out_specs,
        input_output_aliases={5: 0} if first else {},
        scratch_shapes=[
            pltpu.VMEM((narrow, width), own.dtype),
            pltpu.SemaphoreType.DMA((pieces,)),
        ],
        compiler_params=pltpu.CompilerParams(vmem_limit_bytes=16 << 20),
        cost_estimate=pl.CostEstimate(
            flops=4 * narrow * narrow * width, bytes_accessed=8 * narrow * width, transcendentals=0
        ),
    )(counts, own_w, other_w, own, got, *more)


def halves(snapshots, counts, room=17, per=2):
    slots = snapshots.shape[1]
    scale = math.sqrt(slots * lax.axis_size("row"))
    own, own_top, got, top, r_factor, own_w, other_w, load = exchange_and_factor(
        snapshots, counts, scale, room, per
    )
    form = functools.partial(form_basis, counts, own_w, other_w)
    basis, r_factor, load = form(own, got, 0, slots, r_factor, load)
    top = lax.cond(
        load[0, 0] > room, lambda kept: resend(snapshots, kept.shape[1]), lambda kept: kept, top
    )
    (basis,) = form(own_top, top, own.shape[1], slots, basis)
    return (basis, r_factor)


def two_halves(mesh):
    return mesh.shape["snap"] == 2 and mesh.shape["row"] == 16


def solution(mesh):
    placed = (P("snap", "row"), P("row"))
    body = halves if two_halves(mesh) else shards
    return jax.shard_map(
        body, mesh=mesh, in_specs=placed, out_specs=(P("snap", "row"), P()), check_vma=False
    )
```

```python
import functools
import math

import jax
import jax.numpy as jnp
from jax import lax
from jax.experimental import pallas as pl
from jax.experimental.pallas import tpu as pltpu
from jax.sharding import PartitionSpec as P

MESH = pl.DeviceIdType.MESH
HIGH = lax.Precision.HIGHEST
LANES = 128
SUBLANES = 8


def gram_of(block):
    return lax.dot_general(
        block, block, (((1,), (1,)), ((), ())), preferred_element_type=jnp.float32
    )


def factors(gram, scale):
    lower = jnp.linalg.cholesky(gram)
    r_factor = lower.T / scale
    width = gram.shape[0]
    inverse = lax.linalg.triangular_solve(
        lower, jnp.eye(width, dtype=jnp.float32), left_side=True, lower=True
    ).T
    weights = (inverse * scale).astype(jnp.bfloat16)
    return (r_factor, weights)


def apply_weights(weights, block):
    return lax.dot_general(
        weights, block, (((0,), (0,)), ((), ())), preferred_element_type=jnp.float32
    ).astype(jnp.bfloat16)


def shards(snapshots, counts):
    narrow, slots = snapshots.shape
    slot = lax.broadcasted_iota(jnp.int32, (1, slots), 1)
    live = jnp.where(slot < counts[0], snapshots, jnp.zeros_like(snapshots))
    scale = math.sqrt(slots * lax.axis_size("row"))
    whole = lax.all_gather(live, "snap", axis=0, tiled=True)
    gram = lax.psum(gram_of(whole), "row")
    r_factor, weights = factors(gram, scale)
    start = lax.axis_index("snap") * narrow
    own_weights = lax.dynamic_slice_in_dim(weights, start, narrow, 1)
    basis = apply_weights(own_weights, whole)
    return (basis, r_factor)


def mxu_nt(a, b):
    return lax.dot_general(
        a, b, (((1,), (1,)), ((), ())), preferred_element_type=jnp.float32
    )


def eliminate(groups):
    shape = groups[0].shape
    tall = shape[0]
    lane = lax.broadcasted_iota(jnp.int32, shape, 1)
    sub = lax.broadcasted_iota(jnp.int32, shape, 0)
    groups = list(groups)
    count = len(groups)

    def line(block, p):
        return jnp.broadcast_to(block[p:p + 1, :], shape)

    for g in range(count):
        columns = [
            [
                jnp.broadcast_to(groups[v][:, g * tall + q:g * tall + q + 1], shape)
                for v in range(g, count)
            ]
            for q in range(tall)
        ]
        for p in range(tall):
            here = lane == g * tall + p
            pivot = line(columns[p][0], p)
            root = lax.rsqrt(pivot)
            root = root * (1.5 - 0.5 * pivot * root * root)
            lefts = [column * root for column in columns[p]]
            lefts[0] = jnp.where(sub > p, lefts[0], 0.0)
            for q in range(p + 1, tall):
                top = line(columns[q][0], p) * root
                columns[q] = [c - m * top for c, m in zip(columns[q], lefts)]
            row = jnp.where(here, root, line(groups[g], p) * root)
            for v in range(g, count):
                old = groups[v]
                new = jnp.where(here, 0.0, old) - lefts[v - g] * row
                if v == g:
                    new = jnp.where(sub == p, row, jnp.where(sub > p, new, old))
                groups[v] = new
    return groups


def factor_body(scale, gram_ref, r_ref, own_ref, other_ref, work, roots):
    narrow = gram_ref.shape[2]
    rows = narrow // 2
    snap = lax.axis_index("snap")
    row = lax.broadcasted_iota(jnp.int32, (narrow, narrow), 0)
    col = lax.broadcasted_iota(jnp.int32, (narrow, narrow), 1)

    def gram(i):
        here = slice(i * rows, (i + 1) * rows)
        return jnp.concatenate([gram_ref[0, here, :], gram_ref[1, here, :]], axis=0)

    def dot(a, b, dims):
        return lax.dot_general(
            a, b, (dims, ((), ())), precision=HIGH, preferred_element_type=jnp.float32
        )

    def diagonal(which):
        full = work[which]
        inverse = jnp.where(col <= row, full, 0.0)
        upper = jnp.where(col > row, full, 0.0)
        upper = jnp.where(col == row, 1.0 / full, upper)
        return inverse, upper

    work[0] = gram(0)
    work[1] = gram(1)

    @pl.loop(0, 2)
    def _(block):
        groups = [
            work[block, SUBLANES * v:SUBLANES * (v + 1), :] for v in range(narrow // SUBLANES)
        ]
        for v, group in enumerate(eliminate(groups)):
            work[block, SUBLANES * v:SUBLANES * (v + 1), :] = group

        @pl.when(block == 0)
        def _():
            inverse, _ = diagonal(0)
            right = dot(inverse, gram(2), ((1,), (0,)))
            roots[...] = right
            work[1] = work[1] - dot(right, right, ((0,), (0,)))

    inverse0, upper0 = diagonal(0)
    inverse1, upper1 = diagonal(1)
    right = roots[...]
    below = -dot(inverse1, dot(right, inverse0, ((0,), (0,))), ((1,), (0,)))
    r_ref[0:narrow, 0:narrow] = upper0 / scale
    r_ref[0:narrow, narrow:] = right / scale
    r_ref[narrow:, 0:narrow] = jnp.zeros_like(right)
    r_ref[narrow:, narrow:] = upper1 / scale
    own = jnp.where(snap == 0, inverse0, inverse1)
    own_ref[...] = (own * scale).astype(own_ref.dtype)
    other = jnp.where(snap == 0, 0.0, below)
    other_ref[...] = (other * scale).astype(other_ref.dtype)


def meet(sem, stage, chip_row, core):
    y, z = lax.rem(chip_row, 2), lax.div(chip_row, 2)
    last = lax.axis_size("row") // 4 - 1

    def signal(chip):
        pl.semaphore_signal(
            sem.at[stage], inc=1, device_id={"row": 2 * chip + core}, device_id_type=MESH
        )

    signal(chip_row + 1 - 2 * y)

    @pl.when(z > 0)
    def _():
        signal(chip_row - 2)

    @pl.when(z < last)
    def _():
        signal(chip_row + 2)


def meetings(chip_row):
    z = lax.div(chip_row, 2)
    last = lax.axis_size("row") // 4 - 1
    return 1 + jnp.where(z > 0, 1, 0) + jnp.where(z < last, 1, 0)


def panel_kernel(
    units, mid, per, room, scale, counts_ref, x_ref,
    own_low, own_top, got, top, r_ref, own_w_ref, other_w_ref, load_ref,
    mine, near, summed, theirs, part, parts, gram_ref, work, roots,
    tally, tally_s, loose, packed, back,
    load_sem, send_sem, recv_sem, met, near_send, near_recv, sum_send, sum_recv,
    part_send, part_recv, out_send, out_recv, tally_send, tally_recv, tally_copy,
    loose_send, loose_recv, loose_copy, pack_send, pack_recv, back_send, back_recv,
):
    snap = lax.axis_index("snap")
    me = lax.axis_index("row")
    n = lax.axis_size("row")
    core, chip = lax.rem(me, 2), lax.div(me, 2)
    chips = n // 2
    other = {"snap": 1 - snap}
    pair = {"row": me + 1 - 2 * core}
    narrow, slots = x_ref.shape
    step = slots // units
    base = got.shape[1]
    low = base // step
    count = counts_ref[0]
    rows = narrow // 2
    y, z = lax.rem(chip, 2), lax.div(chip, 2)
    last = chips // 2 - 1

    barrier = pltpu.get_barrier_semaphore()

    def greet(device):
        pl.semaphore_signal(barrier, inc=1, device_id=device, device_id_type=MESH)

    greet(other)
    greet(pair)
    greet({"row": 2 * (chip + 1 - 2 * y) + core})

    @pl.when(z > 0)
    def _():
        greet({"row": me - 4})

    @pl.when(z < last)
    def _():
        greet({"row": me + 4})

    tally[me] = jnp.full(tally.shape[1:], count, jnp.int32)
    wide = 8
    span = slots // wide
    loads = []
    for c in range(wide):
        at = pl.ds(c * span, span)
        into, start = (own_low, c * span) if c * span < base else (own_top, c * span - base)
        copy = pltpu.make_async_copy(
            x_ref.at[:, at], into.at[:, pl.ds(start, span)], load_sem.at[c]
        )
        copy.start()
        loads.append(copy)

    pl.semaphore_wait(barrier, 2 + meetings(chip))

    def bulk(u):
        into, start = (got, u * step) if u < low else (top, (u - low) * step)
        return pltpu.make_async_remote_copy(
            src_ref=x_ref.at[:, pl.ds(u * step, step)], dst_ref=into.at[:, pl.ds(start, step)],
            send_sem=send_sem.at[u], recv_sem=recv_sem.at[u],
            device_id=other, device_id_type=MESH,
        )

    def arrived(u):
        if u < low:
            return got[:, u * step:(u + 1) * step]
        return top[:, (u - low) * step:(u - low + 1) * step]

    def send(which, first, stop):
        @pl.when(snap == which)
        def _():
            for u in range(first, stop):
                bulk(u).start()

    ahead = 6
    behind = ahead + 5
    send(0, 0, ahead)
    send(1, mid, mid + ahead)

    for stage in range(met.shape[0]):
        meet(met, stage, chip, core)
        pl.semaphore_wait(met.at[stage], meetings(chip))

    def tally_to(d):
        return pltpu.make_async_remote_copy(
            src_ref=tally.at[me], dst_ref=tally.at[me],
            send_sem=tally_send.at[d - 1], recv_sem=tally_recv.at[d - 1],
            device_id={"row": lax.rem(me + d, n)}, device_id_type=MESH,
        )

    for d in range(1, n):
        tally_to(d).start()

    def loose_to(d, q):
        at = (d - 1) * per + q
        return pltpu.make_async_remote_copy(
            src_ref=x_ref.at[:, pl.ds(base + LANES * (d + n * q), LANES)],
            dst_ref=loose.at[me + n * q],
            send_sem=loose_send.at[at], recv_sem=loose_recv.at[at],
            device_id={"row": lax.rem(me + d, n)}, device_id_type=MESH,
        )

    def loose_own(q):
        return pltpu.make_async_copy(
            x_ref.at[:, pl.ds(base + LANES * n * q, LANES)], loose.at[me + n * q],
            loose_copy.at[q],
        )

    hops = [(d, q) for q in range(per) for d in range(1, n)]

    @pl.when(snap == 0)
    def _():
        for d, q in hops:
            loose_to(d, q).start()
        for q in range(per):
            loose_own(q).start()

    def masked(block, start):
        lane = lax.broadcasted_iota(jnp.int32, block.shape, 1) + start
        return jnp.where(lane < count, block, jnp.zeros_like(block))

    def owned(start, size):
        if start < base:
            return own_low[:, start:start + size]
        return own_top[:, start - base:start - base + size]

    total = jnp.zeros((narrow, narrow), jnp.float32)
    for c in range(wide):
        loads[c].wait()
        block = owned(c * span, span)
        total = total + mxu_nt(masked(block, c * span), block)
    mine[0] = total

    def sum_copy(i):
        away = pltpu.make_async_remote_copy(
            src_ref=mine.at[i, pl.ds(pl.multiple_of((1 - core) * rows, SUBLANES), rows)],
            dst_ref=near.at[i],
            send_sem=near_send.at[i], recv_sem=near_recv.at[i],
            device_id=pair, device_id_type=MESH,
        )
        away.start()
        away.wait()
        kept = mine[i, pl.ds(pl.multiple_of(core * rows, SUBLANES), rows), :]
        summed[i] = kept + near[i]
        return pltpu.make_async_remote_copy(
            src_ref=summed.at[i], dst_ref=theirs.at[i],
            send_sem=sum_send.at[i], recv_sem=sum_recv.at[i],
            device_id=other, device_id_type=MESH,
        )

    diagonal = sum_copy(0)
    diagonal.start()
    send(0, ahead, behind)
    send(1, mid + ahead, units)
    mine[1] = jnp.zeros((narrow, narrow), jnp.float32)

    def cross(first, stop):
        for u in range(first, stop):
            bulk(u).wait_recv()
            block = masked(owned(u * step, step), u * step)

            @pl.when(snap == 1)
            def _():
                mine[1] = mine[1] + mxu_nt(arrived(u), block)

            @pl.when(snap == 0)
            def _():
                mine[1] = mine[1] + mxu_nt(block, arrived(u))

    def learn():
        for d in range(1, n):
            tally_to(d).wait_recv()
        copy = pltpu.make_async_copy(tally, tally_s, tally_copy)
        copy.start()
        copy.wait()
        seen, before = jnp.int32(0), []
        for q in range(per):
            for i in range(n):
                rel = lax.rem(me - i + n, n)
                live = (base + LANES * (rel + n * q) < tally_s[i, 0, 0]).astype(jnp.int32)
                before.append(seen)
                seen = seen + live
        return before, before[1:] + [seen]

    def note_load():
        lane = lax.broadcasted_iota(jnp.int32, tally.shape[1:], 1)
        full = jnp.zeros(tally.shape[1:], jnp.int32)
        for i in range(n):
            rel = jnp.where(lane >= i, lane - i, lane - i + n)
            for q in range(per):
                full = full + jnp.where(base + LANES * (rel + n * q) < tally[i], 1, 0)
        full = jnp.where(lane < n, full, 0).astype(jnp.float32)
        load_ref[0, 0] = jnp.max(full)

    def pack_to(h):
        size = (room // 2, room - room // 2)[h]
        at = pl.ds(h * (room // 2), size)
        return pltpu.make_async_remote_copy(
            src_ref=packed.at[0, at], dst_ref=packed.at[1, at],
            send_sem=pack_send.at[h], recv_sem=pack_recv.at[h],
            device_id=other, device_id_type=MESH,
        )

    def back_to(d, q):
        at = (d - 1) * per + q
        home = lax.rem(me + n - d, n)
        return pltpu.make_async_remote_copy(
            src_ref=back.at[home + n * q],
            dst_ref=top.at[:, pl.ds(LANES * (d + n * q), LANES)],
            send_sem=back_send.at[at], recv_sem=back_recv.at[at],
            device_id={"row": home}, device_id_type=MESH,
        )

    @pl.when(snap == 0)
    def _():
        cross(mid, mid + 9)
        _, after = learn()
        for q in range(per):
            loose_own(q).wait()
        for d, q in hops:
            loose_to(d, q).wait_recv()
        for p in range(room):
            pick = jnp.int32(0)
            for passed in after:
                pick = pick + (passed <= p).astype(jnp.int32)
            pick = jnp.minimum(pick, per * n - 1)
            packed[0, p] = loose[pick]
        for h in range(2):
            pack_to(h).start()
        for u in range(behind, mid + 1):
            bulk(u).start()
        note_load()
        cross(mid + 9, units)

    split = len(hops) // 2

    @pl.when(snap == 1)
    def _():
        cross(0, 8)
        before, _ = learn()
        cross(8, behind)
        for h in range(2):
            pack_to(h).wait_recv()
        for f, place in enumerate(before):
            place = jnp.minimum(place, room - 1)
            back[f] = packed[1, place]
        for d, q in hops[:split]:
            back_to(d, q).start()
        for q in range(per):
            top[:, LANES * n * q:LANES * (n * q + 1)] = back[me + n * q]
        note_load()
        cross(behind, mid)

    crossed = sum_copy(1)
    crossed.start()
    send(0, mid + 1, low)

    diagonal.wait()
    part[0:rows, :] = jnp.where(snap == 0, summed[0], theirs[0])
    part[rows:2 * rows, :] = jnp.where(snap == 0, theirs[0], summed[0])
    crossed.wait()
    part[2 * rows:3 * rows, :] = summed[1] + theirs[1]

    lines = part.shape[0] // chips

    def at(i):
        return pl.ds(pl.multiple_of(i * lines, SUBLANES), lines)

    copies = []
    for d in range(1, chips):
        peer = lax.rem(chip + d, chips)
        copy = pltpu.make_async_remote_copy(
            src_ref=part.at[at(peer)], dst_ref=parts.at[d - 1],
            send_sem=part_send.at[d - 1], recv_sem=part_recv.at[d - 1],
            device_id={"row": 2 * peer + core}, device_id_type=MESH,
        )
        copy.start()
        copies.append(copy)
    total = part[at(chip), :]
    for d in range(1, chips):
        copies[d - 1].wait_recv()
        total = total + parts[d - 1]
    gram_ref[core, at(chip), :] = total
    results = []
    for d in range(1, n):
        peer = lax.rem(me + d, n)
        copy = pltpu.make_async_remote_copy(
            src_ref=gram_ref.at[core, at(chip)], dst_ref=gram_ref.at[core, at(chip)],
            send_sem=out_send.at[d - 1], recv_sem=out_recv.at[d - 1],
            device_id={"row": peer}, device_id_type=MESH,
        )
        copy.start()
        results.append(copy)

    for copy in copies:
        copy.wait_send()
    for copy in results:
        copy.wait()

    @pl.when(snap == 1)
    def _():
        for d, q in hops[split:]:
            back_to(d, q).start()

    factor_body(scale, gram_ref, r_ref, own_w_ref, other_w_ref, work, roots)

    for d in range(1, n):
        tally_to(d).wait_send()

    @pl.when(snap == 0)
    def _():
        for h in range(2):
            pack_to(h).wait_send()
        for d, q in hops:
            loose_to(d, q).wait_send()
        for u in range(low):
            bulk(u).wait_send()

    @pl.when(snap == 1)
    def _():
        for u in range(mid, units):
            bulk(u).wait_send()
        for d, q in hops:
            back_to(d, q).wait()
        for u in range(mid, low):
            bulk(u).wait_recv()


def exchange_and_factor(snapshots, counts, scale, room, per, units=32):
    narrow, slots = snapshots.shape
    dtype = snapshots.dtype
    n = lax.axis_size("row")
    chips = n // 2
    rows = narrow // 2
    height = 3 * rows
    tail = per * n * LANES
    f32 = jnp.float32
    vmem = pl.BlockSpec(memory_space=pltpu.VMEM)
    smem = pl.BlockSpec(memory_space=pltpu.SMEM)
    dma = pltpu.SemaphoreType.DMA
    return pl.pallas_call(
        functools.partial(panel_kernel, units, 14, per, room, scale),
        name="exchange_and_factor",
        out_shape=(
            jax.ShapeDtypeStruct((narrow, slots - tail), dtype),
            jax.ShapeDtypeStruct((narrow, tail), dtype),
            jax.ShapeDtypeStruct((narrow, slots - tail), dtype),
            jax.ShapeDtypeStruct((narrow, tail), dtype),
            jax.ShapeDtypeStruct((2 * narrow, 2 * narrow), f32),
            jax.ShapeDtypeStruct((narrow, narrow), dtype),
            jax.ShapeDtypeStruct((narrow, narrow), dtype),
            jax.ShapeDtypeStruct((1, 1), f32),
        ),
        in_specs=[smem, pl.BlockSpec(memory_space=pltpu.HBM)],
        out_specs=(vmem, vmem, vmem, vmem, vmem, vmem, vmem, smem),
        scratch_shapes=[
            pltpu.VMEM((2, narrow, narrow), f32),
            pltpu.VMEM((2, rows, narrow), f32),
            pltpu.VMEM((2, rows, narrow), f32),
            pltpu.VMEM((2, rows, narrow), f32),
            pltpu.VMEM((height, narrow), f32),
            pltpu.VMEM((chips - 1, height // chips, narrow), f32),
            pltpu.VMEM((2, height, narrow), f32),
            pltpu.VMEM((2, narrow, narrow), f32),
            pltpu.VMEM((narrow, narrow), f32),
            pltpu.VMEM((n, 1, LANES), jnp.int32),
            pltpu.SMEM((n, 1, LANES), jnp.int32),
            pltpu.VMEM((per * n, narrow, LANES), dtype),
            pltpu.VMEM((2, room, narrow, LANES), dtype),
            pltpu.VMEM((per * n, narrow, LANES), dtype),
            dma((8,)),
            dma((units,)),
            dma((units,)),
            pltpu.SemaphoreType.REGULAR((4,)),
            dma((2,)),
            dma((2,)),
            dma((2,)),
            dma((2,)),
            dma((chips - 1,)),
            dma((chips - 1,)),
            dma((n - 1,)),
            dma((n - 1,)),
            dma((n - 1,)),
            dma((n - 1,)),
            dma,
            dma((per * (n - 1),)),
            dma((per * (n - 1),)),
            dma((per,)),
            dma((2,)),
            dma((2,)),
            dma((per * (n - 1),)),
            dma((per * (n - 1),)),
        ],
        compiler_params=pltpu.CompilerParams(
            collective_id=0, has_side_effects=True, vmem_limit_bytes=44 << 20
        ),
    )(counts, snapshots)


def resend_kernel(x_ref, top_ref, send_sem, recv_sem):
    snap = lax.axis_index("snap")
    other = {"snap": 1 - snap}
    start = x_ref.shape[1] - top_ref.shape[1]
    barrier = pltpu.get_barrier_semaphore()
    pl.semaphore_signal(barrier, inc=1, device_id=other, device_id_type=MESH)
    pl.semaphore_wait(barrier, 1)
    copy = pltpu.make_async_remote_copy(
        src_ref=x_ref.at[:, pl.ds(start, top_ref.shape[1])], dst_ref=top_ref,
        send_sem=send_sem, recv_sem=recv_sem, device_id=other, device_id_type=MESH,
    )
    copy.start()
    copy.wait()


def resend(snapshots, tail):
    return pl.pallas_call(
        resend_kernel,
        name="resend",
        out_shape=jax.ShapeDtypeStruct((snapshots.shape[0], tail), snapshots.dtype),
        in_specs=[pl.BlockSpec(memory_space=pl.ANY)],
        out_specs=pl.BlockSpec(memory_space=pl.ANY),
        scratch_shapes=[pltpu.SemaphoreType.DMA, pltpu.SemaphoreType.DMA],
        compiler_params=pltpu.CompilerParams(collective_id=1, has_side_effects=True),
    )(snapshots)


def basis_kernel(first, pieces, counts_ref, own_w, other_w, own_ref, got_ref, *rest):
    if first == 0:
        r_in, out_ref, r_out, stage, sems = rest
    else:
        _, out_ref, stage, sems = rest
    snap = lax.axis_index("snap")
    step = own_ref.shape[1] // pieces
    count = counts_ref[0]

    def piece(c):
        return pltpu.make_async_copy(
            stage.at[:, pl.ds(c * step, step)], out_ref.at[:, pl.ds(first + c * step, step)],
            sems.at[c],
        )

    def form(weights, block, c):
        value = lax.dot_general(
            weights, block, (((1,), (0,)), ((), ())), preferred_element_type=jnp.float32
        )
        lane = lax.broadcasted_iota(jnp.int32, value.shape, 1) + first + c * step
        value = jnp.where(lane < count, value, 0.0).astype(stage.dtype)
        stage[:, c * step:(c + 1) * step] = value
        piece(c).start()

    @pl.when(snap == 0)
    def _():
        weights = own_w[...]
        for c in range(pieces):
            form(weights, own_ref[:, c * step:(c + 1) * step], c)

    @pl.when(snap == 1)
    def _():
        weights = jnp.concatenate([own_w[...], other_w[...]], axis=1)
        for c in range(pieces):
            here = slice(c * step, (c + 1) * step)
            form(weights, jnp.concatenate([own_ref[:, here], got_ref[:, here]], axis=0), c)

    if first == 0:
        r_out[...] = r_in[...]
    for c in range(pieces):
        piece(c).wait()


def form_basis(counts, own_w, other_w, own, got, first, slots, *more, step=2048):
    narrow, width = own.shape
    pieces = width // step
    vmem = pl.BlockSpec(memory_space=pltpu.VMEM)
    smem = pl.BlockSpec(memory_space=pltpu.SMEM)
    hbm = pl.BlockSpec(memory_space=pltpu.HBM)
    out_shape = [jax.ShapeDtypeStruct((narrow, slots), own.dtype)]
    out_specs = [hbm]
    if first == 0:
        out_shape += [jax.ShapeDtypeStruct(m.shape, m.dtype) for m in more]
        out_specs += [vmem]
        more_specs = [vmem]
    else:
        more_specs = [hbm]
    return pl.pallas_call(
        functools.partial(basis_kernel, first, pieces),
        name="form_basis",
        out_shape=out_shape,
        in_specs=[smem, vmem, vmem, vmem, vmem, *more_specs],
        out_specs=out_specs,
        input_output_aliases={5: 0} if first else {},
        scratch_shapes=[
            pltpu.VMEM((narrow, width), own.dtype),
            pltpu.SemaphoreType.DMA((pieces,)),
        ],
        compiler_params=pltpu.CompilerParams(vmem_limit_bytes=16 << 20),
        cost_estimate=pl.CostEstimate(
            flops=4 * narrow * narrow * width, bytes_accessed=8 * narrow * width, transcendentals=0
        ),
    )(counts, own_w, other_w, own, got, *more)


def halves(snapshots, counts, room=17, per=2):
    slots = snapshots.shape[1]
    scale = math.sqrt(slots * lax.axis_size("row"))
    own, own_top, got, top, r_factor, own_w, other_w, load = exchange_and_factor(
        snapshots, counts, scale, room, per
    )
    form = functools.partial(form_basis, counts, own_w, other_w)
    basis, r_factor = form(own, got, 0, slots, r_factor)
    basis, load = lax.optimization_barrier((basis, load))
    top = lax.cond(
        load[0, 0] > room, lambda kept: resend(snapshots, kept.shape[1]), lambda kept: kept, top
    )
    (basis,) = form(own_top, top, own.shape[1], slots, basis)
    return (basis, r_factor)


def two_halves(mesh):
    return mesh.shape["snap"] == 2 and mesh.shape["row"] == 16


def solution(mesh):
    placed = (P("snap", "row"), P("row"))
    body = halves if two_halves(mesh) else shards
    return jax.shard_map(
        body, mesh=mesh, in_specs=placed, out_specs=(P("snap", "row"), P()), check_vma=False
    )
```
